32 devices in a mesh: group: 4 (over x, core), ctx: 8 (over z, y).
Axes of the slice: x: 2, y: 2, z: 4, core: 2. Of those that a mesh axis runs over, the one named last changes fastest.
Arguments:
- query_rows: bfloat16 [4, 2048, 4096], P('group', 'ctx'), may hold values from -250 to 250
- key_rows: bfloat16 [4, 2048, 512], P('group', 'ctx'), may hold values from -7 to 7
- value_rows: bfloat16 [4, 2048, 512], P('group', 'ctx'), may hold values from -6 to 6
- documents: int32 [4, 2048], P('group', 'ctx'), may hold values from 0 to 3, never falling along the last dimension, each value on 1 to 1280 neighbouring positions
- owners: int32 [4, 64, 1], P('group', 'ctx'), may hold values from 0 to 3; in each aligned block of 8 rows (0 to 7, 8 to 15, ..., all dimensions but the last counted through in order) at most 2 rows name the same one
Outputs:
- attended: bfloat16 [4, 2048, 4096], P('group', 'ctx')
- page_pool: bfloat16 [4, 64, 2, 128, 128], P('group', 'ctx')
- page_scales: bfloat16 [4, 64, 2], P('group', 'ctx')
The draws below stay inside these ranges and needn't reach their ends.
Inputs may be any that keep to these rules, and one draw needn't show every extreme that they name: `documents`: document numbers never fall along a group's tokens; each document has at most 1280 tokens. `owners`: among the pages of one device, no owner is named more than 2 times.
All inputs are finite; a program needn't handle non-finite values.
Results may differ from the reference program's by a relative error of at most 0.0028.
Values may be sent and summed in bfloat16 or wider, within the bound.
A program may use at most 128 MiB of HBM per device.

```python
import math
import jax
import jax.numpy as jnp
import numpy as np
from jax import lax

E = 128
HQ = 32
HK = 4
PAGE = 128
TOK_DEV = 256
DOCS = 4
SEQ = 2048
LONGEST = 1280
GROUPS = 4
PAGES = 64
MOST = 2
POOL = 64
N_GROUP = 4
N_CTX = 8


def drawn_pair(key):
    base_key = jax.random.fold_in(key, 7101)
    subkeys = jax.random.split(base_key, 2)
    repeat = HQ // HK
    key_part = jnp.clip(1.6 * jax.random.normal(subkeys[0], (GROUPS, SEQ, HK, E), jnp.float32), -7.0, 7.0)
    query_part = jnp.clip(1.6 * jax.random.normal(subkeys[1], (GROUPS, SEQ, HK, repeat, E), jnp.float32), -7.0, 7.0)
    return (query_part.reshape(GROUPS, SEQ, HQ * E), key_part.reshape(GROUPS, SEQ, HK * E))


def draw_query_rows(key, part):
    return drawn_pair(key)[0].astype(jnp.bfloat16)


def draw_key_rows(key, part):
    return drawn_pair(key)[1].astype(jnp.bfloat16)


def shard_levels(rng, dims, cuts, smallest, high):
    loudness, own = 1.0, jax.random.fold_in(rng, 6)
    for dim, parts in cuts:
        draws = jnp.exp(jax.random.uniform(jax.random.fold_in(own, dim), (parts,), jnp.float32, smallest / len(cuts), high / len(cuts)))
        loudness = loudness * jnp.repeat(draws, dims[dim] // parts).reshape([-1 if axis == dim else 1 for axis in range(len(dims))])
    return loudness


def profile(number_of, total, bound, lean):
    weights = [(1 << 20) // math.isqrt(grade ** lean) + 1 for grade in range(2, number_of + 1)]
    rest, counts = total - bound - (number_of - 1), [1] * (number_of - 1)
    while rest > 0:
        candidates = [i for i in range(number_of - 1) if counts[i] < bound]
        whole, remaining = sum([weights[i] for i in candidates]), rest
        for i in candidates:
            extra = min(bound - counts[i], max(1, remaining * weights[i] // whole), rest)
            counts[i] = counts[i] + extra
            rest = rest - extra
    return np.array([bound] + counts)


def uneven(rng, count, total, bound, skew):
    if count == 2:
        one = jax.random.randint(rng, (), max(1, total - bound), min(bound, total - 1) + 1)
        return jnp.stack([one, total - one])
    tallies = jnp.asarray(profile(count, total, bound, skew), jnp.int32)
    couples = (count - 1) // 2
    source_of, taker = tallies[1:1 + 2 * couples:2], tallies[2:2 + 2 * couples:2]
    margin = jnp.minimum(source_of - 1, bound - taker)
    passed = jax.random.randint(jax.random.fold_in(rng, 1), (couples,), 0, 1 << 20) % (margin + 1)
    tallies = tallies.at[1:1 + 2 * couples:2].set(source_of - passed).at[2:2 + 2 * couples:2].set(taker + passed)
    return tallies[jax.random.permutation(jax.random.fold_in(rng, 2), count)]


def assign_block(own_key, own, number, rows, count, top, most, skew):
    ranking = jax.random.permutation(own_key, count)
    heavy_load, common = shares(count, rows * top, most, skew, True), shares(count, rows * top, most, skew, False)
    places = jnp.arange(count)

    def named(tallies, rotation):
        used = int((tallies > 0).sum())
        fixed = max(1, used // 4)
        moved = fixed + (places - fixed + rotation * (used - fixed)) % max(1, count - fixed)
        return jnp.zeros((count,), jnp.int32).at[ranking[jnp.where(places < fixed, places, moved)]].set(jnp.asarray(tallies, jnp.int32))

    tallies = jnp.where(number % 4 == 0, named(heavy_load, number // 4), named(common, number - number // 4 - 1))
    mixed = jax.random.permutation(jax.random.fold_in(own, 3), count)
    source_of, receiver = mixed[0:count // 2 * 2:2], mixed[1:count // 2 * 2:2]
    room = jnp.minimum(tallies[source_of] - 1, most - tallies[receiver]) // 2
    room = jnp.where((source_of == ranking[0]) | (receiver == ranking[0]) | (tallies[receiver] == 0), 0, jnp.maximum(room, 0))
    moved = jax.random.randint(jax.random.fold_in(own, 4), (count // 2,), 0, 1 << 20) % (room + 1)
    tallies = tallies.at[source_of].add(-moved).at[receiver].add(moved)
    labels = jnp.searchsorted(jnp.cumsum(tallies), jnp.arange(rows * top), side="right").astype(jnp.int32)
    table = labels.reshape(top, rows).T
    table = table[jax.random.permutation(jax.random.fold_in(own, 1), rows)]
    rotation = jax.random.randint(jax.random.fold_in(own, 2), (rows, 1), 0, top)
    return jnp.take_along_axis(table, (jnp.arange(top)[None, :] + rotation) % top, axis=1)


def shares(amount, total, most, skew, full):
    weights = [(1 << 20) // math.isqrt(grade ** skew) + 1 for grade in range(1, amount + 1)]
    largest = most if full else min(most, max(-(-total // amount), total * weights[0] // sum(weights)))
    least = 1 if total - largest >= amount - 1 else 0
    holding, rest = [largest] + [least] * (amount - 1), total - largest - least * (amount - 1)
    while rest > 0:
        candidates = [i for i in range(1, amount) if holding[i] < largest] or [i for i in range(1, amount) if holding[i] < most]
        mass, remaining = sum([weights[i] for i in candidates]), rest
        for i in candidates:
            addition = min(most - holding[i], max(1, remaining * weights[i] // mass), rest)
            holding[i] = holding[i] + addition
            rest = rest - addition
    return np.array(holding)


def centred(key, dims, deviation, bound, cuts=(), kind=jnp.bfloat16):
    array = jax.random.normal(key, dims, jnp.float32) * deviation
    if len(cuts) > 0:
        array = shard_levels(key, dims, cuts, -0.22, 0.18) * array
    return jnp.clip(array, min=-bound, max=bound).astype(kind)


def setup_inputs(seed: int = 0) -> dict:
    key_of = jax.random.split(jax.random.key(seed), 6)
    query_rows = draw_query_rows(jax.random.fold_in(key_of[5], 71), 0)
    key_rows = draw_key_rows(jax.random.fold_in(key_of[5], 71), 0)
    value_rows = centred(key_of[2], (GROUPS, SEQ, HK * E), 1.0, 6.0, ((0, 4), (1, 8)))
    documents = jax.vmap(lambda own: jnp.searchsorted(jnp.cumsum(uneven(own, DOCS, SEQ, LONGEST, 2)), jnp.arange(SEQ), side="right"))(jax.random.split(key_of[3], GROUPS)).reshape((GROUPS, SEQ)).astype(jnp.int32)
    owners_keys = jax.random.split(jax.random.fold_in(key_of[4], 1), GROUPS * PAGES // (TOK_DEV // PAGE * HK))
    owners_turns = jax.random.permutation(jax.random.fold_in(key_of[4], 3), GROUPS * PAGES // (TOK_DEV // PAGE * HK))
    owners = jax.vmap(lambda own, number: assign_block(jax.random.fold_in(key_of[4], 2), own, number, TOK_DEV // PAGE * HK, N_GROUP, 1, MOST, 2))(owners_keys, owners_turns).reshape((GROUPS, PAGES, 1))
    return dict(query_rows=query_rows, key_rows=key_rows, value_rows=value_rows, documents=documents, owners=owners)


epsilon = 1e-06

def attend_group(query_one, key_one, value_one, doc_one):
    repeat = HQ // HK
    score_scale = 1.0 / math.sqrt(E)
    grouped = query_one.reshape(SEQ, HK, repeat, E).astype(jnp.float32)
    key_heads = key_one.reshape(SEQ, HK, E).astype(jnp.float32)
    value_heads = value_one.reshape(SEQ, HK, E).astype(jnp.float32)
    block_rows = math.gcd(SEQ, 512)
    positions = jnp.arange(SEQ, dtype=jnp.int32)

    def one_block(block_index):
        first_row = block_index * block_rows
        query_block = lax.dynamic_slice_in_dim(grouped, first_row, block_rows, 0)
        doc_block = lax.dynamic_slice_in_dim(doc_one, first_row, block_rows, 0)
        query_pos = first_row + jnp.arange(block_rows, dtype=jnp.int32)
        scores = jnp.einsum('qgre,kge->grqk', query_block, key_heads) * score_scale
        visible = (doc_block[:, None] == doc_one[None, :]) & (query_pos[:, None] >= positions[None, :])
        scores = jnp.where(visible, scores, -jnp.inf)
        largest = lax.optimization_barrier(jnp.max(scores, axis=-1, keepdims=True))
        weights = jnp.exp(scores - largest)
        totals = lax.optimization_barrier(jnp.sum(weights, axis=-1))
        rounded = lax.optimization_barrier(weights.astype(jnp.bfloat16)).astype(jnp.float32)
        weighted = jnp.einsum('grqk,kge->qgre', rounded, value_heads)
        result = weighted / jnp.transpose(totals, (2, 0, 1))[..., None]
        return result.astype(jnp.bfloat16)
    blocks = lax.map(one_block, jnp.arange(SEQ // block_rows, dtype=jnp.int32))
    return blocks.reshape(SEQ, HQ * E)

def page_pairs(key_one, value_one):
    block_count = SEQ // PAGE
    key_pages = key_one.reshape(block_count, PAGE, HK, E).transpose(0, 2, 1, 3)
    value_pages = value_one.reshape(block_count, PAGE, HK, E).transpose(0, 2, 1, 3)
    kv_pairs = jnp.stack([key_pages, value_pages], axis=2).reshape(block_count * HK, 2, PAGE, E)
    magnitude = lax.optimization_barrier(jnp.max(jnp.abs(kv_pairs.astype(jnp.float32)), axis=(2, 3))) + epsilon
    scales = magnitude.astype(jnp.bfloat16)
    stored = (kv_pairs.astype(jnp.float32) / scales.astype(jnp.float32)[:, :, None, None]).astype(jnp.bfloat16)
    return (stored, scales)

def reference(query_rows, key_rows, value_rows, documents, owners):
    attended = jnp.stack([attend_group(query_rows[g], key_rows[g], value_rows[g], documents[g]) for g in range(GROUPS)])
    stored, scales = jax.vmap(page_pairs)(key_rows, value_rows)
    per_device = PAGES // N_CTX
    owner_grid = owners[:, :, 0].reshape(GROUPS, N_CTX, per_device)
    page_order = jnp.arange(per_device, dtype=jnp.int32)
    earlier = (owner_grid[..., :, None] == owner_grid[..., None, :]) & (page_order[None, :] < page_order[:, None])
    page_rank = lax.optimization_barrier(jnp.sum(earlier.astype(jnp.int32), axis=-1))
    source = jnp.broadcast_to(jnp.arange(GROUPS, dtype=jnp.int32)[:, None, None], owner_grid.shape)
    column = jnp.broadcast_to(jnp.arange(N_CTX, dtype=jnp.int32)[None, :, None], owner_grid.shape)
    slot = column * (GROUPS * MOST) + source * MOST + page_rank
    target_group = owner_grid.reshape(-1)
    slot_flat = slot.reshape(-1)
    pool = jnp.zeros((GROUPS, POOL, 2, PAGE, E), jnp.bfloat16)
    pool = pool.at[target_group, slot_flat].set(stored.reshape(GROUPS * PAGES, 2, PAGE, E))
    pool_scales = jnp.zeros((GROUPS, POOL, 2), jnp.bfloat16)
    pool_scales = pool_scales.at[target_group, slot_flat].set(scales.reshape(GROUPS * PAGES, 2))
    return (attended, pool, pool_scales)
```

```python
import functools
import math

import jax
import jax.numpy as jnp
from jax import lax
from jax.experimental import pallas as pl
from jax.experimental.pallas import tpu as pltpu
from jax.sharding import PartitionSpec as P

E = 128
PAGE = 128
DOC_ROWS = 16
epsilon = 1e-06
hidden_score = -1e30
MESH = pl.DeviceIdType.MESH


def window_blocks(length, tokens):
    longest = length * 5 // 8
    return min(length // tokens - 1, (longest - 1 + tokens - 1) // tokens)


def kernel(
    heads, key_heads, ctx_count, groups_n, window, depth,
    query_ref, key_ref, value_ref, doc_ref, owner_ref,
    out_ref, pool_ref, scale_ref,
    kv, query, result, key_aug, value_aug, query_mask, key_mask, causal, packed, packed_scales,
    local_sem, query_sem, out_sem, up_sem, side_sem, recv_sem,
    page_sem, page_recv, scale_sem, scale_recv, page_local,
):
    tokens = query.shape[0]
    per_key = heads // key_heads
    group = lax.axis_index("group")
    ctx = lax.axis_index("ctx")
    column = lax.rem(ctx, 2)
    partner = ctx + 1 - 2 * column
    passed = [k for k in range(2, window + 2, 2)]
    body = 2 * tokens + DOC_ROWS
    length = (window + 1) * tokens

    locals_ = []
    for h in range(key_heads):
        cols = pl.ds(h * E, E)
        locals_.append(pltpu.make_async_copy(key_ref.at[0, :, cols], kv.at[0, h, pl.ds(0, tokens)], local_sem.at[3 * h]))
        locals_.append(pltpu.make_async_copy(value_ref.at[0, :, cols], kv.at[0, h, pl.ds(tokens, tokens)], local_sem.at[3 * h + 1]))
        locals_.append(pltpu.make_async_copy(doc_ref, kv.at[0, h, pl.ds(2 * tokens, DOC_ROWS)], local_sem.at[3 * h + 2]))
    for copy in locals_:
        copy.start()
    query_copy = pltpu.make_async_copy(query_ref.at[0], query, query_sem)
    query_copy.start()

    barrier = pltpu.get_barrier_semaphore()
    for step in range(1, groups_n):
        pl.semaphore_signal(barrier, inc=1, device_id=(lax.rem(group + step, groups_n), ctx), device_id_type=MESH)
    pl.semaphore_signal(barrier, inc=1, device_id=(group, partner), device_id_type=MESH)

    @pl.when(ctx >= 2)
    def _():
        pl.semaphore_signal(barrier, inc=1, device_id=(group, ctx - 2), device_id_type=MESH)

    @pl.when(ctx + 2 < ctx_count)
    def _():
        pl.semaphore_signal(barrier, inc=1, device_id=(group, ctx + 2), device_id_type=MESH)

    greeted = groups_n + jnp.where(ctx >= 2, 1, 0) + jnp.where(ctx + 2 < ctx_count, 1, 0)
    pl.semaphore_wait(barrier, greeted)

    for copy in locals_:
        copy.wait()

    def up_copy(k, h):
        return pltpu.make_async_remote_copy(
            kv.at[k, h], kv.at[k + 2, h], up_sem.at[k, h], recv_sem.at[k + 2, h],
            device_id=(group, ctx + 2), device_id_type=MESH)

    def side_copy(k, h, there):
        return pltpu.make_async_remote_copy(
            kv.at[k, h], kv.at[there, h], side_sem.at[k, h], recv_sem.at[there, h],
            device_id=(group, partner), device_id_type=MESH)

    def each_send(k, h, act):
        here = ctx >= k
        limits = (k + 2 <= window, k + 2 <= window + 1)
        if limits[1]:
            ok = here & (ctx + 2 < ctx_count)
            if not limits[0]:
                ok = ok & (column == 1)

            @pl.when(ok)
            def _():
                act(up_copy(k, h))

        if k + 1 <= window:
            @pl.when(here & (column == 0))
            def _():
                act(side_copy(k, h, k + 1))

        if k >= 2 and k - 1 <= window:
            @pl.when(here & (column == 1))
            def _():
                act(side_copy(k, h, k - 1))

    def arrives(k):
        ok = ctx >= k
        return ok & (column == 1) if k > window else ok

    def await_block(k, h):
        pltpu.make_async_remote_copy(
            kv.at[k, h], kv.at[k, h], up_sem.at[k, h], recv_sem.at[k, h],
            device_id=(group, partner), device_id_type=MESH).wait_recv()

    def pass_on(k, h):
        @pl.when(arrives(k))
        def _():
            await_block(k, h)

        each_send(k, h, lambda copy: copy.start())

    ahead = min(2, key_heads)
    for h in range(ahead):
        each_send(0, h, lambda copy: copy.start())

    for k in range(1, window + 1):
        @pl.when(ctx < k)
        def _(k=k):
            kv[k] = jnp.zeros(kv.shape[1:], kv.dtype)
            kv[k, 0, pl.ds(2 * tokens, DOC_ROWS), :] = jnp.full((DOC_ROWS, E), -1.0, kv.dtype)

    rows = lax.broadcasted_iota(jnp.int32, (tokens, tokens), 0)
    cols = lax.broadcasted_iota(jnp.int32, (tokens, tokens), 1)
    causal[...] = jnp.where(rows >= cols, 0.0, hidden_score)
    lanes = lax.broadcasted_iota(jnp.int32, (E, E), 1).astype(jnp.float32)

    def mark_columns(k, b):
        line = kv[k, 0, pl.ds(2 * tokens, DOC_ROWS), :].astype(jnp.float32)[b:b + 1, :]
        return jnp.transpose(jnp.broadcast_to(line, (E, E)))

    for b in range(tokens // E):
        query_mask[pl.ds(b * E, E), :] = jnp.where(mark_columns(0, b) == lanes, 1.0, 0.0).astype(jnp.bfloat16)

    blocks_n = tokens // PAGE
    page_count = blocks_n * key_heads
    owner = [owner_ref[p] for p in range(page_count)]
    rank = []
    for p in range(page_count):
        r = jnp.int32(0)
        for e in range(p):
            r = r + jnp.where(owner[e] == owner[p], 1, 0)
        rank.append(r)
    line_of = lax.broadcasted_iota(jnp.int32, (8, E), 0)
    for part in range(2):
        for p in range(page_count):
            b, h = p // key_heads, p % key_heads
            page = kv[0, h, pl.ds(part * tokens + b * PAGE, PAGE), :].astype(jnp.float32)
            scale = (jnp.max(jnp.max(jnp.abs(page), axis=0, keepdims=True), axis=1, keepdims=True) + epsilon)
            scale = scale.astype(jnp.bfloat16).astype(jnp.float32)
            stored = (page / scale).astype(jnp.bfloat16).astype(jnp.float32)
            for o in range(groups_n):
                for r in range(depth):
                    chosen = jnp.where((owner[p] == o) & (rank[p] == r), 1.0, 0.0)
                    term = (stored * chosen).astype(jnp.bfloat16)
                    spread = jnp.where(line_of == 2 * r + part, scale * chosen, 0.0)
                    if p == 0:
                        packed[o, r, part] = term
                    else:
                        packed[o, r, part] += term
                    if p == 0 and part == 0 and r == 0:
                        packed_scales[o] = spread
                    else:
                        packed_scales[o] += spread

    for h in range(ahead):
        for k in passed:
            pass_on(k, h)

    def page_copies(step, act):
        to = lax.rem(group + step, groups_n)
        act(pltpu.make_async_remote_copy(
            packed.at[to], pool_ref.at[0, pl.ds(group * depth, depth)], page_sem.at[step], page_recv.at[step],
            device_id=(to, ctx), device_id_type=MESH))
        act(pltpu.make_async_remote_copy(
            packed_scales.at[to], scale_ref.at[group], scale_sem.at[step], scale_recv.at[step],
            device_id=(to, ctx), device_id_type=MESH))

    own_page = pltpu.make_async_copy(packed.at[group], pool_ref.at[0, pl.ds(group * depth, depth)], page_local.at[0])
    own_scale = pltpu.make_async_copy(packed_scales.at[group], scale_ref.at[group], page_local.at[1])

    query_copy.wait()
    factor = math.log2(math.e) / math.sqrt(E)
    pair = 2
    inner = per_key // pair

    def out_copy(h):
        wide = pl.ds(h * per_key * E, per_key * E)
        return pltpu.make_async_copy(result.at[:, wide], out_ref.at[0, :, wide], out_sem.at[h])

    for h in range(key_heads):
        if h + ahead < key_heads:
            each_send(0, h + ahead, lambda copy: copy.start())
        for k in range(1, window + 1):
            if k % 2 == 1:
                @pl.when(ctx >= k)
                def _(k=k):
                    await_block(k, h)
        if h == 0:
            for k in range(window + 1):
                for b in range(tokens // E):
                    key_mask[pl.ds(k * tokens + b * E, E), :] = jnp.where(
                        mark_columns(k, b) == lanes, 0.0, hidden_score).astype(jnp.bfloat16)
            key_aug[:, pl.ds(E, E)] = key_mask[...]
            value_aug[:, pl.ds(E, E)] = jnp.ones((length, E), jnp.bfloat16)
        for k in range(window + 1):
            key_aug[pl.ds(k * tokens, tokens), pl.ds(0, E)] = kv[k, h, pl.ds(0, tokens), :]
            value_aug[pl.ds(k * tokens, tokens), pl.ds(0, E)] = kv[k, h, pl.ds(tokens, tokens), :]

        def one_pair(i, carry):
            if h + ahead < key_heads:
                for n, k in enumerate(passed):
                    @pl.when(i == n % inner)
                    def _(k=k):
                        pass_on(k, h + ahead)
            for j in range(pair):
                at = pl.ds(pl.multiple_of((h * per_key + i * pair + j) * E, E), E)
                wide = jnp.concatenate([query[:, at], query_mask[...]], axis=1)
                scores = lax.dot_general(wide, key_aug[...], (((1,), (1,)), ((), ())),
                                         preferred_element_type=jnp.float32)
                near = scores[:, :tokens] + causal[...]
                far = scores[:, tokens:]
                largest = jnp.maximum(jnp.max(near, axis=1, keepdims=True), jnp.max(far, axis=1, keepdims=True))
                weights = jnp.concatenate(
                    [jnp.exp2((near - largest) * factor).astype(jnp.bfloat16),
                     jnp.exp2((far - largest) * factor).astype(jnp.bfloat16)], axis=1)
                summed = jnp.dot(weights, value_aug[...], preferred_element_type=jnp.float32)
                result[:, at] = (summed[:, :E] / summed[:, E:]).astype(jnp.bfloat16)
            return carry

        lax.fori_loop(0, inner, one_pair, 0)
        out_copy(h).start()
        if h == 0:
            own_page.start()
            own_scale.start()
            for step in range(1, groups_n):
                page_copies(step, lambda copy: copy.start())

    for h in range(key_heads):
        for k in [0] + passed:
            each_send(k, h, lambda copy: copy.wait_send())
    for step in range(1, groups_n):
        page_copies(step, lambda copy: copy.wait())
    own_page.wait()
    own_scale.wait()
    for h in range(key_heads):
        out_copy(h).wait()


def local(query_rows, key_rows, value_rows, documents, owners):
    tokens = query_rows.shape[1]
    heads = query_rows.shape[2] // E
    key_heads = key_rows.shape[2] // E
    ctx_count = lax.axis_size("ctx")
    groups_n = lax.axis_size("group")
    window = window_blocks(tokens * ctx_count, tokens)
    page_count = owners.shape[1]
    depth = max(2, (page_count + groups_n - 1) // groups_n)
    marks = documents[0].astype(jnp.bfloat16).reshape(tokens // E, E)
    marks = jnp.pad(marks, ((0, DOC_ROWS - tokens // E), (0, 0)))
    slots = window + 2
    length = (window + 1) * tokens
    anywhere = pl.BlockSpec(memory_space=pl.ANY)
    attended, pool, scales = pl.pallas_call(
        functools.partial(kernel, heads, key_heads, ctx_count, groups_n, window, depth),
        out_shape=(
            jax.ShapeDtypeStruct(query_rows.shape, jnp.bfloat16),
            jax.ShapeDtypeStruct((1, groups_n * depth, 2, PAGE, E), jnp.bfloat16),
            jax.ShapeDtypeStruct((groups_n, 8, E), jnp.float32),
        ),
        in_specs=[anywhere] * 4 + [pl.BlockSpec(memory_space=pltpu.SMEM)],
        out_specs=(anywhere, anywhere, anywhere),
        scratch_shapes=[
            pltpu.VMEM((slots, key_heads, 2 * tokens + DOC_ROWS, E), jnp.bfloat16),
            pltpu.VMEM((tokens, heads * E), jnp.bfloat16),
            pltpu.VMEM((tokens, heads * E), jnp.bfloat16),
            pltpu.VMEM((length, 2 * E), jnp.bfloat16),
            pltpu.VMEM((length, 2 * E), jnp.bfloat16),
            pltpu.VMEM((tokens, E), jnp.bfloat16),
            pltpu.VMEM((length, E), jnp.bfloat16),
            pltpu.VMEM((tokens, tokens), jnp.float32),
            pltpu.VMEM((groups_n, depth, 2, PAGE, E), jnp.bfloat16),
            pltpu.VMEM((groups_n, 8, E), jnp.float32),
            pltpu.SemaphoreType.DMA((3 * key_heads,)),
            pltpu.SemaphoreType.DMA,
            pltpu.SemaphoreType.DMA((key_heads,)),
            pltpu.SemaphoreType.DMA((slots, key_heads)),
            pltpu.SemaphoreType.DMA((slots, key_heads)),
            pltpu.SemaphoreType.DMA((slots, key_heads)),
            pltpu.SemaphoreType.DMA((groups_n,)),
            pltpu.SemaphoreType.DMA((groups_n,)),
            pltpu.SemaphoreType.DMA((groups_n,)),
            pltpu.SemaphoreType.DMA((groups_n,)),
            pltpu.SemaphoreType.DMA((2,)),
        ],
        compiler_params=pltpu.CompilerParams(
            collective_id=0, has_side_effects=True, vmem_limit_bytes=56 * 1024 * 1024),
        name="attend_and_deliver",
    )(query_rows, key_rows, value_rows, marks, owners[0, :, 0])
    page_scales = scales[:, : 2 * depth, 0].reshape(1, groups_n * depth, 2).astype(jnp.bfloat16)
    return (attended, pool, page_scales)


def solution(mesh):
    placed = (
        P("group", "ctx", None),
        P("group", "ctx", None),
        P("group", "ctx", None),
        P("group", "ctx"),
        P("group", "ctx", None),
    )
    return jax.shard_map(
        local,
        mesh=mesh,
        in_specs=placed,
        out_specs=(
            P("group", "ctx", None),
            P("group", "ctx", None, None, None),
            P("group", "ctx", None),
        ),
        check_vma=False,
    )
```

```python
import functools
import math

import jax
import jax.numpy as jnp
from jax import lax
from jax.experimental import pallas as pl
from jax.experimental.pallas import tpu as pltpu
from jax.sharding import PartitionSpec as P

E = 128
PAGE = 128
DOC_ROWS = 16
epsilon = 1e-06
hidden_score = -1e30
MESH = pl.DeviceIdType.MESH


def window_blocks(length, tokens):
    longest = length * 5 // 8
    return min(length // tokens - 1, (longest - 1 + tokens - 1) // tokens)


def kernel(
    heads, key_heads, ctx_count, groups_n, window, depth,
    query_ref, key_ref, value_ref, doc_ref, owner_ref,
    out_ref, pool_ref, scale_ref,
    kv, marks, query, result, key_aug, value_aug, query_mask, key_mask, causal, packed, packed_scales,
    local_sem, query_sem, out_sem, up_sem, side_sem, recv_sem,
    page_sem, page_recv, scale_sem, scale_recv, page_local,
):
    tokens = query.shape[0]
    per_key = heads // key_heads
    group = lax.axis_index("group")
    ctx = lax.axis_index("ctx")
    column = lax.rem(ctx, 2)
    partner = ctx + 1 - 2 * column
    turn = window - 2 if window % 2 == 1 and window >= 3 else 0
    evens = [k for k in range(2, window + 1, 2)]

    def climbs(col, h):
        return False

    def passed(h):
        late = [turn] if climbs(0, h) or climbs(1, h) else []
        return evens + late + ([window + 1] if window % 2 == 1 and not climbs(0, h) else [])

    def chunk(k, h):
        return kv.at[k, h, pl.ds(0, 2 * tokens + (DOC_ROWS if h == 0 else 0))]

    length = (window + 1) * tokens

    marks[...] = jnp.zeros(marks.shape, marks.dtype)
    for b in range(tokens // E):
        marks[b:b + 1, :] = doc_ref[:, b * E:(b + 1) * E].astype(jnp.float32).astype(jnp.bfloat16)

    locals_ = []
    for h in range(key_heads):
        cols = pl.ds(h * E, E)
        locals_.append(pltpu.make_async_copy(key_ref.at[0, :, cols], kv.at[0, h, pl.ds(0, tokens)], local_sem.at[2 * h]))
        locals_.append(pltpu.make_async_copy(value_ref.at[0, :, cols], kv.at[0, h, pl.ds(tokens, tokens)], local_sem.at[2 * h + 1]))
    for copy in locals_:
        copy.start()
    query_copy = pltpu.make_async_copy(query_ref.at[0], query, query_sem)
    query_copy.start()

    barrier = pltpu.get_barrier_semaphore()
    for step in range(1, groups_n):
        pl.semaphore_signal(barrier, inc=1, device_id=(lax.rem(group + step, groups_n), ctx), device_id_type=MESH)
    pl.semaphore_signal(barrier, inc=1, device_id=(group, partner), device_id_type=MESH)

    @pl.when(ctx >= 2)
    def _():
        pl.semaphore_signal(barrier, inc=1, device_id=(group, ctx - 2), device_id_type=MESH)

    @pl.when(ctx + 2 < ctx_count)
    def _():
        pl.semaphore_signal(barrier, inc=1, device_id=(group, ctx + 2), device_id_type=MESH)

    greeted = groups_n + jnp.where(ctx >= 2, 1, 0) + jnp.where(ctx + 2 < ctx_count, 1, 0)
    pl.semaphore_wait(barrier, greeted)
    mark_copy = pltpu.make_async_copy(marks, kv.at[0, 0, pl.ds(2 * tokens, DOC_ROWS)], local_sem.at[2 * key_heads])
    mark_copy.start()
    mark_copy.wait()

    for copy in locals_:
        copy.wait()

    def up_copy(k, h):
        return pltpu.make_async_remote_copy(
            chunk(k, h), chunk(k + 2, h), up_sem.at[k, h], recv_sem.at[k + 2, h],
            device_id=(group, ctx + 2), device_id_type=MESH)

    def side_copy(k, h, there):
        return pltpu.make_async_remote_copy(
            chunk(k, h), chunk(there, h), side_sem.at[k, h], recv_sem.at[there, h],
            device_id=(group, partner), device_id_type=MESH)

    def each_send(k, h, act):
        here = ctx >= k
        above = here & (ctx + 2 < ctx_count)
        if k % 2 == 1:
            pick = [col for col in range(2) if climbs(col, h)]
            up = above if len(pick) == 2 else above & (column == pick[0])
        elif k + 2 <= window:
            up = above
        elif k + 2 == window + 1 and not climbs(0, h):
            up = above & (column == 1)
        else:
            up = None
        if up is not None:
            @pl.when(up)
            def _():
                act(up_copy(k, h))

        if k % 2 == 0 and k + 1 <= window and not (k + 1 == window and climbs(1, h)):
            @pl.when(here & (column == 0))
            def _():
                act(side_copy(k, h, k + 1))

        if k % 2 == 0 and k >= 2:
            @pl.when(here & (column == 1))
            def _():
                act(side_copy(k, h, k - 1))

    def arrives(k):
        ok = ctx >= k
        return ok & (column == 1) if k > window else ok

    def await_block(k, h):
        pltpu.make_async_remote_copy(
            chunk(k, h), chunk(k, h), up_sem.at[k, h], recv_sem.at[k, h],
            device_id=(group, partner), device_id_type=MESH).wait_recv()

    def pass_on(k, h):
        @pl.when(arrives(k))
        def _():
            await_block(k, h)

        each_send(k, h, lambda copy: copy.start())

    ahead = min(1, key_heads)
    own_ahead = min(2, key_heads)
    for h in range(own_ahead):
        each_send(0, h, lambda copy: copy.start())

    for k in range(1, window + 1):
        @pl.when(ctx < k)
        def _(k=k):
            kv[k] = jnp.zeros(kv.shape[1:], kv.dtype)
            kv[k, 0, pl.ds(2 * tokens, DOC_ROWS), :] = jnp.full((DOC_ROWS, E), -1.0, kv.dtype)

    rows = lax.broadcasted_iota(jnp.int32, (tokens, tokens), 0)
    cols = lax.broadcasted_iota(jnp.int32, (tokens, tokens), 1)
    causal[...] = jnp.where(rows >= cols, 0.0, hidden_score)
    lanes = lax.broadcasted_iota(jnp.int32, (E, E), 1).astype(jnp.float32)

    def mark_columns(k, b):
        line = kv[k, 0, pl.ds(2 * tokens, DOC_ROWS), :].astype(jnp.float32)[b:b + 1, :]
        return jnp.transpose(jnp.broadcast_to(line, (E, E)))

    for b in range(tokens // E):
        query_mask[pl.ds(b * E, E), :] = jnp.where(mark_columns(0, b) == lanes, 1.0, 0.0).astype(jnp.bfloat16)

    for h in range(ahead):
        for k in passed(h):
            pass_on(k, h)

    def pack_pages():
        blocks_n = tokens // PAGE
        page_count = blocks_n * key_heads
        owner = [owner_ref[p] for p in range(page_count)]
        rank = []
        for p in range(page_count):
            r = jnp.int32(0)
            for e in range(p):
                r = r + jnp.where(owner[e] == owner[p], 1, 0)
            rank.append(r)
        line_of = lax.broadcasted_iota(jnp.int32, (8, E), 0)
        for part in range(2):
            for p in range(page_count):
                b, h = p // key_heads, p % key_heads
                page = kv[0, h, pl.ds(part * tokens + b * PAGE, PAGE), :].astype(jnp.float32)
                scale = (jnp.max(jnp.max(jnp.abs(page), axis=0, keepdims=True), axis=1, keepdims=True) + epsilon)
                scale = scale.astype(jnp.bfloat16).astype(jnp.float32)
                stored = (page / scale).astype(jnp.bfloat16).astype(jnp.float32)
                for o in range(groups_n):
                    for r in range(depth):
                        chosen = jnp.where((owner[p] == o) & (rank[p] == r), 1.0, 0.0)
                        term = (stored * chosen).astype(jnp.bfloat16)
                        spread = jnp.where(line_of == 2 * r + part, scale * chosen, 0.0)
                        if p == 0:
                            packed[o, r, part] = term
                        else:
                            packed[o, r, part] += term
                        if p == 0 and part == 0 and r == 0:
                            packed_scales[o] = spread
                        else:
                            packed_scales[o] += spread

    def page_copies(step, act):
        to = lax.rem(group + step, groups_n)
        act(pltpu.make_async_remote_copy(
            packed.at[to], pool_ref.at[0, pl.ds(group * depth, depth)], page_sem.at[step], page_recv.at[step],
            device_id=(to, ctx), device_id_type=MESH))
        act(pltpu.make_async_remote_copy(
            packed_scales.at[to], scale_ref.at[group], scale_sem.at[step], scale_recv.at[step],
            device_id=(to, ctx), device_id_type=MESH))

    own_page = pltpu.make_async_copy(packed.at[group], pool_ref.at[0, pl.ds(group * depth, depth)], page_local.at[0])
    own_scale = pltpu.make_async_copy(packed_scales.at[group], scale_ref.at[group], page_local.at[1])

    query_copy.wait()
    factor = math.log2(math.e) / math.sqrt(E)
    pair = 2
    inner = per_key // pair

    def out_copy(h):
        wide = pl.ds(h * per_key * E, per_key * E)
        return pltpu.make_async_copy(result.at[:, wide], out_ref.at[0, :, wide], out_sem.at[h])

    for h in range(key_heads):
        if h + own_ahead < key_heads:
            each_send(0, h + own_ahead, lambda copy: copy.start())
        for k in range(1, window + 1):
            if k not in passed(h):
                @pl.when(ctx >= k)
                def _(k=k):
                    await_block(k, h)
        if h == 0:
            for k in range(window + 1):
                for b in range(tokens // E):
                    key_mask[pl.ds(k * tokens + b * E, E), :] = jnp.where(
                        mark_columns(k, b) == lanes, 0.0, hidden_score).astype(jnp.bfloat16)
            key_aug[:, pl.ds(E, E)] = key_mask[...]
            value_aug[:, pl.ds(E, E)] = jnp.ones((length, E), jnp.bfloat16)
        for k in range(window + 1):
            key_aug[pl.ds(k * tokens, tokens), pl.ds(0, E)] = kv[k, h, pl.ds(0, tokens), :]
            value_aug[pl.ds(k * tokens, tokens), pl.ds(0, E)] = kv[k, h, pl.ds(tokens, tokens), :]

        def one_pair(i, carry):
            if h + ahead < key_heads:
                for n, k in enumerate(passed(h + ahead)):
                    @pl.when(i == n % inner)
                    def _(k=k):
                        pass_on(k, h + ahead)
            for j in range(pair):
                at = pl.ds(pl.multiple_of((h * per_key + i * pair + j) * E, E), E)
                wide = jnp.concatenate([query[:, at], query_mask[...]], axis=1)
                scores = lax.dot_general(wide, key_aug[...], (((1,), (1,)), ((), ())),
                                         preferred_element_type=jnp.float32)
                near = scores[:, :tokens] + causal[...]
                far = scores[:, tokens:]
                largest = jnp.maximum(jnp.max(near, axis=1, keepdims=True), jnp.max(far, axis=1, keepdims=True))
                weights = jnp.concatenate(
                    [jnp.exp2((near - largest) * factor).astype(jnp.bfloat16),
                     jnp.exp2((far - largest) * factor).astype(jnp.bfloat16)], axis=1)
                summed = jnp.dot(weights, value_aug[...], preferred_element_type=jnp.float32)
                result[:, at] = (summed[:, :E] / summed[:, E:]).astype(jnp.bfloat16)
            return carry

        lax.fori_loop(0, inner, one_pair, 0)
        out_copy(h).start()
        if h == 0:
            pack_pages()
        if h == min(1, key_heads - 1):
            own_page.start()
            own_scale.start()
            for step in range(1, groups_n):
                page_copies(step, lambda copy: copy.start())

    for h in range(key_heads):
        for k in [0] + passed(h):
            each_send(k, h, lambda copy: copy.wait_send())
    for step in range(1, groups_n):
        page_copies(step, lambda copy: copy.wait())
    own_page.wait()
    own_scale.wait()
    for h in range(key_heads):
        out_copy(h).wait()


def local(query_rows, key_rows, value_rows, documents, owners):
    tokens = query_rows.shape[1]
    heads = query_rows.shape[2] // E
    key_heads = key_rows.shape[2] // E
    ctx_count = lax.axis_size("ctx")
    groups_n = lax.axis_size("group")
    window = window_blocks(tokens * ctx_count, tokens)
    page_count = owners.shape[1]
    depth = max(2, (page_count + groups_n - 1) // groups_n)
    slots = window + 2
    length = (window + 1) * tokens
    anywhere = pl.BlockSpec(memory_space=pl.ANY)
    attended, pool, scales = pl.pallas_call(
        functools.partial(kernel, heads, key_heads, ctx_count, groups_n, window, depth),
        out_shape=(
            jax.ShapeDtypeStruct(query_rows.shape, jnp.bfloat16),
            jax.ShapeDtypeStruct((1, groups_n * depth, 2, PAGE, E), jnp.bfloat16),
            jax.ShapeDtypeStruct((groups_n, 8, E), jnp.float32),
        ),
        in_specs=[anywhere] * 3 + [pl.BlockSpec(memory_space=pltpu.VMEM), pl.BlockSpec(memory_space=pltpu.SMEM)],
        out_specs=(anywhere, anywhere, anywhere),
        scratch_shapes=[
            pltpu.VMEM((slots, key_heads, 2 * tokens + DOC_ROWS, E), jnp.bfloat16),
            pltpu.VMEM((DOC_ROWS, E), jnp.bfloat16),
            pltpu.VMEM((tokens, heads * E), jnp.bfloat16),
            pltpu.VMEM((tokens, heads * E), jnp.bfloat16),
            pltpu.VMEM((length, 2 * E), jnp.bfloat16),
            pltpu.VMEM((length, 2 * E), jnp.bfloat16),
            pltpu.VMEM((tokens, E), jnp.bfloat16),
            pltpu.VMEM((length, E), jnp.bfloat16),
            pltpu.VMEM((tokens, tokens), jnp.float32),
            pltpu.VMEM((groups_n, depth, 2, PAGE, E), jnp.bfloat16),
            pltpu.VMEM((groups_n, 8, E), jnp.float32),
            pltpu.SemaphoreType.DMA((2 * key_heads + 1,)),
            pltpu.SemaphoreType.DMA,
            pltpu.SemaphoreType.DMA((key_heads,)),
            pltpu.SemaphoreType.DMA((slots, key_heads)),
            pltpu.SemaphoreType.DMA((slots, key_heads)),
            pltpu.SemaphoreType.DMA((slots, key_heads)),
            pltpu.SemaphoreType.DMA((groups_n,)),
            pltpu.SemaphoreType.DMA((groups_n,)),
            pltpu.SemaphoreType.DMA((groups_n,)),
            pltpu.SemaphoreType.DMA((groups_n,)),
            pltpu.SemaphoreType.DMA((2,)),
        ],
        compiler_params=pltpu.CompilerParams(
            collective_id=0, has_side_effects=True, vmem_limit_bytes=56 * 1024 * 1024),
        name="attend_and_deliver",
    )(query_rows, key_rows, value_rows, documents, owners[0, :, 0])
    page_scales = scales[:, : 2 * depth, 0].reshape(1, groups_n * depth, 2).astype(jnp.bfloat16)
    return (attended, pool, page_scales)


def solution(mesh):
    placed = (
        P("group", "ctx", None),
        P("group", "ctx", None),
        P("group", "ctx", None),
        P("group", "ctx"),
        P("group", "ctx", None),
    )
    return jax.shard_map(
        local,
        mesh=mesh,
        in_specs=placed,
        out_specs=(
            P("group", "ctx", None),
            P("group", "ctx", None, None, None),
            P("group", "ctx", None),
        ),
        check_vma=False,
    )
```
